128 devices in a mesh: seq: 16 (over z, x), tensor: 8 (over y, core).
Axes of the slice: x: 4, y: 4, z: 4, core: 2. Of those that a mesh axis runs over, the one named last changes fastest.
Arguments:
- queries: bfloat16 [16384, 8192], P('seq', 'tensor'), may hold values from -6 to 6
- keys: bfloat16 [16384, 1024], P('seq', 'tensor'), may hold values from -6 to 6
- values: bfloat16 [16384, 1024], P('seq', 'tensor'), may hold values from -6 to 6
- key_blocks: int32 [64, 128, 16], P('tensor'), may hold values from 0 to 127, as said below
- block_counts: int32 [64, 128], P('tensor'), may hold values from 1 to 16, as said below
- out_weight: bfloat16 [8192, 8192], P('tensor'), may hold values from -0.59765625 to 0.59765625
Outputs:
- projected: bfloat16 [16384, 8192], P('seq', 'tensor')
The draws below stay inside these ranges and needn't reach their ends.
Inputs may be any that keep to these rules, and one draw needn't show every extreme that they name: For head h and query block b the first block_counts[h, b] entries of key_blocks[h, b] are different blocks of 0 to b, the first being b itself; the later entries are block numbers without meaning. block_counts[h, b] is at most b + 1; the last query block of every head has exactly 16.
All inputs are finite; a program needn't handle non-finite values.
Results may differ from the reference program's by a relative error of at most 0.014.
Values may be sent and summed in bfloat16 or wider, within the bound.
No kernel may reach another device: no remote copies, remote signals or barrier semaphores. Data moves between devices by JAX's collectives and lax.ppermute only.
A program may use at most 128 MiB of HBM per device.

```python
import jax
import jax.numpy as jnp
from jax import lax

D = 8192
HEADS = 64
KV_HEADS = 8
HEAD_DIM = 128
BLOCK = 128
KMAX = 16
SEQ = 16384
NB = 128
HQ_DEV = 8
N_TENSOR = 8


def draw_queries(key, part):
    base = jnp.clip(jax.random.normal(jax.random.fold_in(key, 1), (SEQ, HEADS * HEAD_DIM), jnp.float32), -6.0, 6.0)
    return base.astype(jnp.bfloat16)


def draw_keys(key, part):
    base = jnp.clip(jax.random.normal(jax.random.fold_in(key, 3), (SEQ, KV_HEADS * HEAD_DIM), jnp.float32), -6.0, 6.0)
    return base.astype(jnp.bfloat16)


def mask_layout(key):
    base = jax.random.fold_in(key, 29)
    rows = jnp.arange(NB, dtype=jnp.int32)
    density = jax.random.randint(jax.random.fold_in(base, 1), (HEADS, 1), 1, 5)
    cap = 1 + (KMAX - 1) * (rows[None, :] + 1) * density // (NB * 4)
    low = jnp.maximum(1, cap // 2)
    counts = jax.random.randint(jax.random.fold_in(base, 2), (HEADS, NB), low, cap + 1)
    counts = jnp.minimum(counts, rows[None, :] + 1)
    counts = jnp.where(rows[None, :] == NB - 1, KMAX, counts).astype(jnp.int32)
    kind = jax.random.randint(jax.random.fold_in(base, 3), (HEADS, 1, 1), 0, 2)
    vertical = jax.random.randint(jax.random.fold_in(base, 4), (HEADS, 1, NB), 0, 4) == 0
    slash_set = jax.random.randint(jax.random.fold_in(base, 5), (HEADS, NB), 0, 4) == 0
    slash_set = slash_set | (rows[None, :] == 1)
    offsets = jnp.mod(rows[:, None] - rows[None, :], NB)
    slash_hit = slash_set[:, offsets]
    scattered = jax.random.randint(jax.random.fold_in(base, 6), (HEADS, NB, NB), 0, 3) == 0
    noise = jax.random.randint(jax.random.fold_in(base, 7), (HEADS, NB, NB), 0, 1000)
    pattern = jnp.where(kind == 0, 2000 * vertical.astype(jnp.int32) + 2000 * slash_hit.astype(jnp.int32), 2000 * scattered.astype(jnp.int32))
    valid = (rows[None, None, :] <= rows[None, :, None]).astype(jnp.int32)
    diagonal = (rows[None, None, :] == rows[None, :, None]).astype(jnp.int32)
    score = valid * (200000 + noise + pattern) + diagonal * 200000
    distinct = score * NB + rows[None, None, :]
    slots = lax.top_k(distinct, KMAX)[1].astype(jnp.int32)
    return (slots, counts)


def draw_key_blocks(key, part):
    return mask_layout(key)[0]


def draw_block_counts(key, part):
    return mask_layout(key)[1]


def with_spikes(entries, key, source, target, blocks, factor):
    def block_of(position):
        return (jnp.arange(entries.shape[position]) // (entries.shape[position] // blocks)).reshape((-1,) + (1,) * (entries.ndim - 1 - position))

    one_side = jax.random.permutation(key, blocks)[block_of(target)]
    second = (block_of(target) + blocks // 2) % blocks
    return jnp.where((block_of(source) == one_side) | (block_of(source) == second), factor * entries, entries)


def block_scale(own_key, dims, split, smallest, high):
    loudness = 1.0
    for dim, blocks in split:
        heights = jax.random.uniform(jax.random.fold_in(jax.random.fold_in(own_key, 6), dim), (blocks,), jnp.float32, smallest / len(split), high / len(split))
        loudness = loudness * jnp.repeat(jnp.exp(heights), dims[dim] // blocks).reshape((-1,) + (1,) * (len(dims) - 1 - dim))
    return loudness


def centred(own_key, shape, deviation, bound, split=(), kind=jnp.bfloat16):
    factor_of = block_scale(own_key, shape, split, -0.22, 0.18) if split else 1.0
    result = jax.random.normal(own_key, shape, jnp.float32) * deviation * factor_of
    return jnp.minimum(jnp.maximum(result, -bound), bound).astype(kind)


def noise_with(own_key, dims, deviation, limit, pieces, heavy, held_as=jnp.bfloat16):
    array = deviation * jax.random.normal(own_key, dims, jnp.float32)
    if pieces:
        array = array * block_scale(own_key, dims, pieces, -0.22, 0.18)
    return jnp.clip(with_spikes(array, jax.random.fold_in(own_key, 3), *heavy), -limit, limit).astype(held_as)


def setup_inputs(seed: int = 0) -> dict:
    splits = jax.random.split(jax.random.key(seed), 7)
    queries = draw_queries(jax.random.fold_in(splits[6], 71), 0)
    keys = draw_keys(jax.random.fold_in(splits[6], 71), 0)
    values = centred(splits[2], (SEQ, KV_HEADS * HEAD_DIM), 1.0, 6.0, ((0, 16), (1, 8)))
    key_blocks = draw_key_blocks(jax.random.fold_in(splits[6], 71), 0)
    block_counts = draw_block_counts(jax.random.fold_in(splits[6], 71), 0)
    out_weight = noise_with(splits[5], (HEADS * HEAD_DIM, D), 0.1, 0.59765625, ((0, 8),), (0, 1, 8, 2.0))
    return {"queries": queries, "keys": keys, "values": values, "key_blocks": key_blocks, "block_counts": block_counts, "out_weight": out_weight}


neg_large = -1.0e30


def reference(queries, keys, values, key_blocks, block_counts, out_weight):
    seq_len = queries.shape[0]
    nblocks = seq_len // BLOCK
    ratio = HEADS // KV_HEADS
    softmax_scale = HEAD_DIM ** -0.5
    q_all = queries.reshape(nblocks, BLOCK, HEADS, HEAD_DIM)
    k_all = keys.reshape(nblocks, BLOCK, KV_HEADS, HEAD_DIM)
    v_all = values.reshape(nblocks, BLOCK, KV_HEADS, HEAD_DIM)
    q_pos = jnp.arange(BLOCK, dtype=jnp.int32)[:, None]
    k_pos = jnp.arange(BLOCK, dtype=jnp.int32)[None, :]
    block_ids = jnp.arange(nblocks, dtype=jnp.int32)
    slot_ids = jnp.arange(KMAX, dtype=jnp.int32)

    def one_head(head):
        group = head // ratio
        query_per_head = lax.dynamic_index_in_dim(q_all, head, 2, keepdims=False).astype(jnp.float32)
        k_head = lax.dynamic_index_in_dim(k_all, group, 2, keepdims=False).astype(jnp.float32)
        v_head = lax.dynamic_index_in_dim(v_all, group, 2, keepdims=False).astype(jnp.float32)
        slots = lax.dynamic_index_in_dim(key_blocks, head, 0, keepdims=False)
        counts = lax.dynamic_index_in_dim(block_counts, head, 0, keepdims=False)
        selected_key_rows = k_head[slots]
        selected_value_rows = v_head[slots]
        logit_scores = jnp.einsum("imh,itzh->imtz", query_per_head, selected_key_rows) * softmax_scale
        slot_used = slot_ids[None, :] < counts[:, None]
        earlier = slots < block_ids[:, None]
        visible = slot_used[:, None, :, None] & (earlier[:, None, :, None] | (q_pos >= k_pos)[None, :, None, :])
        masked = jnp.where(visible, logit_scores, neg_large)
        top = jnp.max(masked, axis=(2, 3))
        weights = jnp.where(visible, jnp.exp(masked - top[:, :, None, None]), 0.0)
        total = jnp.sum(weights, axis=(2, 3))
        rounded_output = lax.optimization_barrier(weights.astype(jnp.bfloat16)).astype(jnp.float32)
        summed_heads = jnp.einsum("xuin,xinw->xuw", rounded_output, selected_value_rows)
        return (summed_heads / total[:, :, None]).astype(jnp.bfloat16)

    attended = lax.map(one_head, jnp.arange(HEADS, dtype=jnp.int32))
    attended = attended.transpose(1, 2, 0, 3).reshape(seq_len, HEADS * HEAD_DIM)
    width = HQ_DEV * HEAD_DIM
    groups = attended.reshape(seq_len, N_TENSOR, width).transpose(1, 0, 2)
    weight_groups = out_weight.reshape(N_TENSOR, width, D)

    def add_group(total, pair):
        part = jnp.dot(pair[0], pair[1], preferred_element_type=jnp.float32)
        part = lax.optimization_barrier(part.astype(jnp.bfloat16)).astype(jnp.float32)
        return total + part, None

    summed_heads, _ = lax.scan(add_group, jnp.zeros((seq_len, D), jnp.float32), (groups, weight_groups))
    return summed_heads.astype(jnp.bfloat16)
```

```python
import functools
import math

import jax
import jax.numpy as jnp
from jax import lax
from jax.experimental import pallas as pl
from jax.experimental.pallas import tpu as pltpu
from jax.sharding import PartitionSpec as P

HEAD_DIM = 128
BLOCK = 128
SIDE = 4
CORES = 2
PARTS = 10
BLOCKS = 2
VARIANTS = (1, 2, 3, 4, 6, 8)
ORDER = (2, 1, 3, 0)
NEG = -1e30


def along_x(step):
    return [(z * SIDE + x, z * SIDE + (x + step) % SIDE) for z in range(SIDE) for x in range(SIDE)]


def along_z(step):
    return [(z * SIDE + x, (z + step) % SIDE * SIDE + x) for z in range(SIDE) for x in range(SIDE)]


def along_y(step):
    return [(y * CORES + c, (y + step) % SIDE * CORES + c) for y in range(SIDE) for c in range(CORES)]


def other_core():
    return [(y * CORES + c, y * CORES + CORES - 1 - c) for y in range(SIDE) for c in range(CORES)]


def ring(piece, perm):
    half = piece.shape[0] // 2
    before = lax.ppermute(piece, "seq", perm(1))
    after = lax.ppermute(piece, "seq", perm(-1))
    far_low = lax.ppermute(before[:half], "seq", perm(1))
    far_high = lax.ppermute(after[half:], "seq", perm(-1))
    return before, after, far_low, far_high


def gather(piece, first, second):
    line = ring(piece, first)
    near = (piece,) + ring(piece, second)
    rest = jnp.concatenate(line, 0)
    rest = (rest,) + ring(rest, second)
    parts = []
    for one, more in zip(near[:3], rest[:3]):
        parts += [one, more]
    return parts + list(near[3:]) + list(rest[3:]), line[0]


def attend_first_kernel(kmax, tab, q_ref, *refs):
    parts, (o_ref, k_all, v_all), sem = refs[: 2 * PARTS], refs[2 * PARTS : -1], refs[-1]
    copies = []
    for some, whole in ((parts[:PARTS], k_all), (parts[PARTS:], v_all)):
        at = 0
        for part in some:
            copies.append(pltpu.make_async_copy(part, whole.at[pl.ds(at, part.shape[0])], sem.at[len(copies)]))
            at += part.shape[0]
    for copy in copies:
        copy.start()
    for copy in copies:
        copy.wait()
    attend_kernel(kmax, tab, q_ref, k_all, v_all, o_ref)


def attend_kernel(kmax, tab, q_ref, k_all, v_all, o_ref):
    heads = q_ref.shape[1] // HEAD_DIM
    units = q_ref.shape[0] // BLOCK * heads
    counts_at, keys_at, values_at = units, 2 * units, 2 * units + units * kmax
    scale = HEAD_DIM ** -0.5 * math.log2(math.e)
    rows = lax.broadcasted_iota(jnp.int32, (BLOCK, BLOCK), 0)
    cols = lax.broadcasted_iota(jnp.int32, (BLOCK, BLOCK), 1)
    causal = rows >= cols

    def block_of(ref, slot):
        return ref[pl.ds(pl.multiple_of(slot * BLOCK, BLOCK), BLOCK), :]

    def unit_scores(unit, pairs):
        head, local = unit % heads, unit // heads
        q = q_ref[
            pl.ds(pl.multiple_of(local * BLOCK, BLOCK), BLOCK),
            pl.ds(pl.multiple_of(head * HEAD_DIM, HEAD_DIM), HEAD_DIM),
        ]
        count = tab[counts_at + unit]
        scores = []
        for pair in range(pairs):
            two = jnp.concatenate(
                [block_of(k_all, tab[keys_at + unit * kmax + 2 * pair + i]) for i in range(2)], 0
            )
            both = lax.dot_general(q, two, (((1,), (1,)), ((), ())), preferred_element_type=jnp.float32)
            for i in range(2):
                j = 2 * pair + i
                one = both[:, i * BLOCK : (i + 1) * BLOCK]
                if j == 0:
                    one = jnp.where(causal, one, NEG)
                else:
                    one = one + jnp.where(j < count, 0.0, NEG).astype(jnp.float32)
                scores.append(one)
        return scores

    def unit_weights(scores):
        top = functools.reduce(jnp.maximum, scores)
        top = jnp.max(top, axis=1, keepdims=True)
        weights = [jnp.exp2((one - top) * scale) for one in scores]
        total = functools.reduce(jnp.add, weights)
        total = jnp.sum(total, axis=1, keepdims=True)
        return [one.astype(jnp.bfloat16) for one in weights], total

    def unit_finish(unit, weights, total):
        head, local = unit % heads, unit // heads
        values = jnp.concatenate(
            [block_of(v_all, tab[values_at + unit * kmax + j]) for j in range(len(weights))], 0
        )
        acc = jnp.dot(jnp.concatenate(weights, 1), values, preferred_element_type=jnp.float32)
        o_ref[
            pl.ds(pl.multiple_of(local * BLOCK, BLOCK), BLOCK),
            pl.ds(pl.multiple_of(head * HEAD_DIM, HEAD_DIM), HEAD_DIM),
        ] = (acc / total).astype(jnp.bfloat16)

    def step(group, carry):
        members = [tab[2 * group + i] for i in range(2)]
        most = jnp.maximum(tab[counts_at + members[0]], tab[counts_at + members[1]])
        need = (most + 1) // 2
        fewer = 0
        for pairs in VARIANTS:

            @pl.when((need > fewer) & (need <= pairs))
            def _():
                scores = [unit_scores(unit, pairs) for unit in members]
                ready = [unit_weights(one) for one in scores]
                for unit, (weights, total) in zip(members, ready):
                    unit_finish(unit, weights, total)

            fewer = pairs
        return carry

    lax.fori_loop(0, units // 2, step, 0)


def in_hbm(array):
    return pltpu.with_memory_space_constraint(array, pltpu.HBM)


def in_vmem(array):
    return pltpu.with_memory_space_constraint(array, pltpu.VMEM)


def attend(table, queries, kmax, k_parts, v_parts):
    rows, width = queries.shape
    tokens = sum(part.shape[0] for part in k_parts)
    vmem = pl.BlockSpec(memory_space=pltpu.VMEM)
    smem = pl.BlockSpec(memory_space=pltpu.SMEM)
    pairs = rows // BLOCK * (width // HEAD_DIM) * kmax // 2
    cost = pl.CostEstimate(
        flops=pairs * 4 * BLOCK * BLOCK * HEAD_DIM,
        bytes_accessed=4 * tokens * HEAD_DIM + 4 * rows * width,
        transcendentals=pairs * BLOCK * BLOCK,
    )
    params = pltpu.CompilerParams(vmem_limit_bytes=8 << 20)
    out = jax.ShapeDtypeStruct((rows, width), jnp.bfloat16)
    if len(k_parts) > 1:
        whole = pltpu.VMEM((tokens, HEAD_DIM), jnp.bfloat16)
        return pl.pallas_call(
            functools.partial(attend_first_kernel, kmax),
            out_shape=[out, whole, whole],
            in_specs=[smem, vmem] + [pl.BlockSpec(memory_space=pltpu.HBM)] * (2 * PARTS),
            out_specs=[vmem] * 3,
            scratch_shapes=[pltpu.SemaphoreType.DMA((2 * PARTS,))],
            compiler_params=params,
            cost_estimate=cost,
            name="attend_first",
        )(table, queries, *map(in_hbm, k_parts), *map(in_hbm, v_parts))
    return pl.pallas_call(
        functools.partial(attend_kernel, kmax),
        out_shape=out,
        in_specs=[smem, vmem, vmem, vmem],
        out_specs=vmem,
        compiler_params=params,
        cost_estimate=cost,
        name="attend",
    )(table, queries, in_vmem(k_parts[0]), in_vmem(v_parts[0]))


def tables(key_blocks, block_counts, seq_index, local_blocks):
    start = seq_index * local_blocks
    lists = lax.dynamic_slice_in_dim(key_blocks, start, local_blocks, 1)
    counts = lax.dynamic_slice_in_dim(block_counts, start, local_blocks, 1)
    source = lists // local_blocks
    within = lists % local_blocks

    def place(step):
        step = step % SIDE
        return jnp.where(step == 0, 0, jnp.where(step == SIDE - 1, 1, jnp.where(step == 1, 2, 3)))

    z_place = place(source // SIDE - seq_index // SIDE)
    x_place = place(source % SIDE - seq_index % SIDE)
    key_at = (z_place * SIDE + x_place) * local_blocks + within
    value_at = (x_place * SIDE + z_place) * local_blocks + within
    counts, key_at, value_at = (jnp.moveaxis(one, 1, 0) for one in (counts, key_at, value_at))
    chunks = local_blocks // BLOCKS
    counts, key_at, value_at = (one.reshape(chunks, -1) for one in (counts, key_at, value_at))
    order = jnp.argsort(counts, axis=1).astype(jnp.int32)
    table = jnp.concatenate([order, counts, key_at, value_at], 1)
    return lax.optimization_barrier([table[i] for i in range(chunks)])


def product_kernel(steps, cols, a_ref, b_ref, w_ref, v_ref, *refs):
    outs, (both, left, w_buf, sem) = refs[:-4], refs[-4:]
    rows, depth = a_ref.shape
    width = w_buf.shape[2]
    half = rows // 2
    strip = 2 * depth // sem.shape[1]

    def copies(k):
        source = pl.ds(pl.multiple_of(cols[ORDER.index(steps[0]) + k] * width, width), width)
        return [
            pltpu.make_async_copy(
                one.at[pl.ds(i * strip, strip), source],
                w_buf.at[k, pl.ds(which * depth + i * strip, strip), :],
                sem.at[k, which * (depth // strip) + i],
            )
            for which, one in enumerate((w_ref, v_ref))
            for i in range(depth // strip)
        ]

    for k in range(len(steps)):
        for copy in copies(k):
            copy.start()
    left[:, :depth] = a_ref[...]
    left[:, depth:] = b_ref[...]

    def run(k, carry):
        for copy in copies(k):
            copy.wait()
        both[...] = jnp.dot(left[...], w_buf[k], preferred_element_type=jnp.float32)
        for index, step in enumerate(steps):

            @pl.when(k == index)
            def _():
                if step == 0:
                    outs[0][...] = both[...]
                elif step == 2:
                    outs[0][:half, :] = both[:half, :].astype(jnp.bfloat16)
                    outs[1][:half, :] = both[half:, :].astype(jnp.bfloat16)
                elif step == 1:
                    outs[0][half:, :] = both[half:, :].astype(jnp.bfloat16)
                    outs[2][...] = both[:half, :]
                else:
                    outs[1][half:, :] = both[:half, :].astype(jnp.bfloat16)
                    outs[3][...] = both[half:, :]

        return carry

    lax.fori_loop(0, len(steps), run, 0)


def product(steps, cols, attended, swapped, weight, theirs):
    rows, depth = attended.shape
    width = weight.shape[1] // (SIDE * CORES)
    half = rows // 2
    if steps == (0,):
        shapes = [((rows, width), jnp.float32)]
    else:
        shapes = [((rows, width), jnp.bfloat16)] * 2 + [((half, width), jnp.float32)] * 2
    vmem = pl.BlockSpec(memory_space=pltpu.VMEM)
    hbm = pl.BlockSpec(memory_space=pltpu.HBM)
    return pl.pallas_call(
        functools.partial(product_kernel, steps),
        out_shape=[jax.ShapeDtypeStruct(s, d) for s, d in shapes],
        in_specs=[pl.BlockSpec(memory_space=pltpu.SMEM), vmem, vmem, hbm, hbm],
        out_specs=[vmem] * len(shapes),
        scratch_shapes=[
            pltpu.VMEM((rows, width), jnp.float32),
            pltpu.VMEM((rows, 2 * depth), jnp.bfloat16),
            pltpu.VMEM((len(steps), 2 * depth, width), jnp.bfloat16),
            pltpu.SemaphoreType.DMA((len(steps), 8)),
        ],
        compiler_params=pltpu.CompilerParams(vmem_limit_bytes=(8 + 4 * len(steps)) << 20),
        cost_estimate=pl.CostEstimate(
            flops=4 * rows * depth * width * len(steps),
            bytes_accessed=8 * rows * width + 4 * depth * width * len(steps),
            transcendentals=0,
        ),
        name="product",
    )(cols, attended, swapped, in_hbm(weight), in_hbm(theirs))


def after(value, *others):
    return lax.optimization_barrier((value,) + others)[0]


def body(queries, keys, values, key_blocks, block_counts, out_weight):
    tokens = queries.shape[0]
    seq_index = lax.axis_index("seq")
    tensor_index = lax.axis_index("tensor")
    y, core = tensor_index // CORES, tensor_index % CORES
    kmax = key_blocks.shape[2]
    k_parts, k_line = gather(keys, along_x, along_z)
    v_parts, v_line = gather(values, along_z, along_x)
    plans = tables(key_blocks, block_counts, seq_index, tokens // BLOCK)

    cols = jnp.stack([(y + step) % SIDE * CORES + core for step in ORDER]).astype(jnp.int32)
    theirs = lax.ppermute(after(out_weight, k_line, v_line), "tensor", other_core())

    def send(piece, step):
        return lax.ppermute(piece, "tensor", along_y(step))

    def finish(own, up, down, up_low, down_high):
        half = own.shape[0] // 2
        low = own[:half] + up_low.astype(jnp.float32) + down[half:].astype(jnp.float32)
        high = own[half:] + up[half:].astype(jnp.float32) + down_high.astype(jnp.float32)
        return [low.astype(jnp.bfloat16), high.astype(jnp.bfloat16)]

    results = []
    at = 0
    waiting = None
    rows = BLOCKS * BLOCK
    for plan in plans:
        half = rows // 2
        some = queries[at : at + rows]
        at += rows
        if waiting is None:
            attended, key_all, value_all = attend(plan, some, kmax, k_parts, v_parts)
        else:
            pair, (up, down, up_rest, down_rest) = waiting
            plan = after(plan, up_rest)
            attended = attend(plan, some, kmax, [key_all], [value_all])
        swapped = lax.ppermute(attended, "tensor", other_core())
        if waiting is not None:
            up_low = (up_rest + up[:half].astype(jnp.float32)).astype(jnp.bfloat16)
            down_high = (down_rest + down[:half].astype(jnp.float32)).astype(jnp.bfloat16)
            (own,) = product((0,), cols, after(pair[0], attended), pair[1], out_weight, theirs)
            results += finish(own, up, down, send(up_low, 1), send(down_high, -1))
            attended = after(attended, up_low, down_high)
        up, down, up_rest, down_rest = product((2, 1, 3), cols, attended, swapped, out_weight, theirs)
        waiting = (attended, swapped), (send(up, 1), send(down, -1), up_rest, down_rest)
    pair, (up, down, up_rest, down_rest) = waiting
    (own,) = product((0,), cols, pair[0], pair[1], out_weight, theirs)
    up_low = (up_rest + up[:half].astype(jnp.float32)).astype(jnp.bfloat16)
    down_high = (down_rest + down[:half].astype(jnp.float32)).astype(jnp.bfloat16)
    results += finish(own, up, down, send(up_low, 1), send(down_high, -1))
    return jnp.concatenate(results, 0)


def solution(mesh):
    placed = (
        P("seq", "tensor"),
        P("seq", "tensor"),
        P("seq", "tensor"),
        P("tensor", None, None),
        P("tensor", None),
        P("tensor", None),
    )
    return jax.shard_map(
        body, mesh=mesh, in_specs=placed, out_specs=P("seq", "tensor"), check_vma=False
    )
```

```python
import functools
import math

import jax
import jax.numpy as jnp
from jax import lax
from jax.experimental import pallas as pl
from jax.experimental.pallas import tpu as pltpu
from jax.sharding import PartitionSpec as P

HEAD_DIM = 128
BLOCK = 128
SIDE = 4
CORES = 2
PARTS = 8
CHUNKS = (3, 3, 2)
VARIANTS = (1, 2, 3, 4, 6, 8)
ORDER = (2, 1, 3, 0)
COST = 2
NEG = -1e30


def along_x(step):
    return [(z * SIDE + x, z * SIDE + (x + step) % SIDE) for z in range(SIDE) for x in range(SIDE)]


def along_z(step):
    return [(z * SIDE + x, (z + step) % SIDE * SIDE + x) for z in range(SIDE) for x in range(SIDE)]


def along_y(step):
    return [(y * CORES + c, (y + step) % SIDE * CORES + c) for y in range(SIDE) for c in range(CORES)]


def other_core():
    return [(y * CORES + c, y * CORES + CORES - 1 - c) for y in range(SIDE) for c in range(CORES)]


def ring(piece, perm):
    half = piece.shape[0] // 2
    before = lax.ppermute(piece, "seq", perm(1))
    after = lax.ppermute(piece, "seq", perm(-1))
    far_low = lax.ppermute(before[:half], "seq", perm(1))
    far_high = lax.ppermute(after[half:], "seq", perm(-1))
    return before, after, far_low, far_high


def gather(piece, first, second):
    before, behind, far_low, far_high = ring(piece, first)
    low = jnp.concatenate([piece, before], 0)
    high = jnp.concatenate([behind, far_low, far_high], 0)

    def pass_on(part, step):
        return lax.ppermute(part, "seq", second(step))

    low_before, high_behind = pass_on(low, 1), pass_on(high, -1)
    low_behind, high_before = pass_on(low, -1), pass_on(high, 1)
    low_far, high_far = pass_on(low_before, 1), pass_on(high_behind, -1)
    return [low, high, low_before, high_before, low_behind, high_behind, low_far, high_far]


def attend_first_kernel(kmax, tab, q_ref, *refs):
    parts, (o_ref, k_out, v_out), (k_all, v_all, sem) = refs[: 2 * PARTS], refs[2 * PARTS : -3], refs[-3:]
    copies = []
    for some, whole in ((parts[:PARTS], k_all), (parts[PARTS:], v_all)):
        at = 0
        for part in some:
            copies.append(pltpu.make_async_copy(part, whole.at[pl.ds(at, part.shape[0])], sem.at[len(copies)]))
            at += part.shape[0]
    for copy in copies:
        copy.start()
    for copy in copies:
        copy.wait()
    keep = [
        pltpu.make_async_copy(k_all, k_out, sem.at[2 * PARTS]),
        pltpu.make_async_copy(v_all, v_out, sem.at[2 * PARTS + 1]),
    ]
    for copy in keep:
        copy.start()
    attend_kernel(kmax, tab, q_ref, k_all, v_all, o_ref)
    for copy in keep:
        copy.wait()


def attend_kernel(kmax, tab, q_ref, k_all, v_all, o_ref):
    heads = q_ref.shape[1] // HEAD_DIM
    units = q_ref.shape[0] // BLOCK * heads
    counts_at, keys_at, values_at = units, 2 * units, 2 * units + units * kmax
    scale = HEAD_DIM ** -0.5 * math.log2(math.e)
    rows = lax.broadcasted_iota(jnp.int32, (BLOCK, BLOCK), 0)
    cols = lax.broadcasted_iota(jnp.int32, (BLOCK, BLOCK), 1)
    causal = rows >= cols

    def block_of(ref, slot):
        return ref[pl.ds(pl.multiple_of(slot * BLOCK, BLOCK), BLOCK), :]

    def unit_scores(unit, pairs):
        head, local = unit % heads, unit // heads
        q = q_ref[
            pl.ds(pl.multiple_of(local * BLOCK, BLOCK), BLOCK),
            pl.ds(pl.multiple_of(head * HEAD_DIM, HEAD_DIM), HEAD_DIM),
        ]
        count = tab[counts_at + unit]
        scores = []
        for pair in range(pairs):
            two = jnp.concatenate(
                [block_of(k_all, tab[keys_at + unit * kmax + 2 * pair + i]) for i in range(2)], 0
            )
            both = lax.dot_general(q, two, (((1,), (1,)), ((), ())), preferred_element_type=jnp.float32)
            for i in range(2):
                j = 2 * pair + i
                one = both[:, i * BLOCK : (i + 1) * BLOCK]
                if j == 0:
                    one = jnp.where(causal, one, NEG)
                else:
                    one = one + jnp.where(j < count, 0.0, NEG).astype(jnp.float32)
                scores.append(one)
        return scores

    def unit_weights(scores):
        top = functools.reduce(jnp.maximum, scores)
        top = jnp.max(top, axis=1, keepdims=True)
        weights = [jnp.exp2((one - top) * scale) for one in scores]
        total = functools.reduce(jnp.add, weights)
        total = jnp.sum(total, axis=1, keepdims=True)
        return [one.astype(jnp.bfloat16) for one in weights], total

    def unit_finish(unit, weights, total):
        head, local = unit % heads, unit // heads
        values = jnp.concatenate(
            [block_of(v_all, tab[values_at + unit * kmax + j]) for j in range(len(weights))], 0
        )
        acc = jnp.dot(jnp.concatenate(weights, 1), values, preferred_element_type=jnp.float32)
        o_ref[
            pl.ds(pl.multiple_of(local * BLOCK, BLOCK), BLOCK),
            pl.ds(pl.multiple_of(head * HEAD_DIM, HEAD_DIM), HEAD_DIM),
        ] = (acc / total).astype(jnp.bfloat16)

    def step(group, carry):
        members = [tab[2 * group + i] for i in range(2)]
        most = jnp.maximum(tab[counts_at + members[0]], tab[counts_at + members[1]])
        need = (most + 1) // 2
        fewer = 0
        for pairs in VARIANTS:

            @pl.when((need > fewer) & (need <= pairs))
            def _():
                scores = [unit_scores(unit, pairs) for unit in members]
                ready = [unit_weights(one) for one in scores]
                for unit, (weights, total) in zip(members, ready):
                    unit_finish(unit, weights, total)

            fewer = pairs
        return carry

    lax.fori_loop(0, units // 2, step, 0)


def in_hbm(array):
    return pltpu.with_memory_space_constraint(array, pltpu.HBM)


def in_vmem(array):
    return pltpu.with_memory_space_constraint(array, pltpu.VMEM)


def attend(table, queries, kmax, k_parts, v_parts):
    rows, width = queries.shape
    tokens = sum(part.shape[0] for part in k_parts)
    vmem = pl.BlockSpec(memory_space=pltpu.VMEM)
    smem = pl.BlockSpec(memory_space=pltpu.SMEM)
    pairs = rows // BLOCK * (width // HEAD_DIM) * kmax // 2
    declared = cost(pairs * 4 * BLOCK * BLOCK * HEAD_DIM, 4 * tokens * HEAD_DIM + 4 * rows * width)
    gathered = len(k_parts) > 1
    params = pltpu.CompilerParams(vmem_limit_bytes=(20 if gathered else 8) << 20)
    out = jax.ShapeDtypeStruct((rows, width), jnp.bfloat16)
    if gathered:
        hbm = pl.BlockSpec(memory_space=pltpu.HBM)
        whole = pltpu.HBM((tokens, HEAD_DIM), jnp.bfloat16)
        held = pltpu.VMEM((tokens, HEAD_DIM), jnp.bfloat16)
        return pl.pallas_call(
            functools.partial(attend_first_kernel, kmax),
            out_shape=[out, whole, whole],
            in_specs=[smem, vmem] + [hbm] * (2 * PARTS),
            out_specs=[vmem, hbm, hbm],
            scratch_shapes=[held, held, pltpu.SemaphoreType.DMA((2 * PARTS + 2,))],
            compiler_params=params,
            cost_estimate=declared,
            name="attend_first",
        )(table, queries, *map(in_hbm, k_parts), *map(in_hbm, v_parts))
    return pl.pallas_call(
        functools.partial(attend_kernel, kmax),
        out_shape=out,
        in_specs=[smem, vmem, vmem, vmem],
        out_specs=vmem,
        compiler_params=params,
        cost_estimate=declared,
        name="attend",
    )(table, queries, in_vmem(k_parts[0]), in_vmem(v_parts[0]))


def tables(key_blocks, block_counts, seq_index, local_blocks):
    heads, _, kmax = key_blocks.shape
    start = seq_index * local_blocks
    lists = lax.dynamic_slice_in_dim(key_blocks, start, local_blocks, 1)
    counts = lax.dynamic_slice_in_dim(block_counts, start, local_blocks, 1)
    source = lists // local_blocks
    within = lists % local_blocks

    def place(step):
        step = step % SIDE
        return jnp.where(step == 0, 0, jnp.where(step == SIDE - 1, 1, jnp.where(step == 1, 2, 3)))

    z_place = place(source // SIDE - seq_index // SIDE)
    x_place = place(source % SIDE - seq_index % SIDE)
    key_at = (z_place * SIDE + x_place) * local_blocks + within
    value_at = (x_place * SIDE + z_place) * local_blocks + within
    counts, key_at, value_at = (jnp.moveaxis(one, 1, 0) for one in (counts, key_at, value_at))
    counts, key_at, value_at = (one.reshape(-1) for one in (counts, key_at, value_at))
    chunk = [index for index, blocks in enumerate(CHUNKS) for _ in range(blocks * heads)]
    order = jnp.argsort(counts + (kmax + 1) * jnp.array(chunk, jnp.int32)).astype(jnp.int32)
    out, at = [], 0
    for blocks in CHUNKS:
        units = slice(at, at + blocks * heads)
        slots = slice(at * kmax, (at + blocks * heads) * kmax)
        out.append(jnp.concatenate([order[units] - at, counts[units], key_at[slots], value_at[slots]], 0))
        at += blocks * heads
    return lax.optimization_barrier(out)


def product_kernel(sends, owns, cols, *refs):
    ins, refs = refs[: 2 * (sends + owns)], refs[2 * (sends + owns) :]
    w_ref, v_ref = refs[:2]
    outs, (both, w_buf, sem), lefts = refs[2 : 2 + 4 * sends + owns], refs[-3:], refs[2 + 4 * sends + owns : -3]
    depth = ins[0].shape[1]
    width = w_buf.shape[2]
    strip = 2 * depth // sem.shape[1]
    first = 0 if sends else 3

    def copies(k):
        source = pl.ds(pl.multiple_of(cols[first + k] * width, width), width)
        return [
            pltpu.make_async_copy(
                one.at[pl.ds(i * strip, strip), source],
                w_buf.at[k, pl.ds(which * depth + i * strip, strip), :],
                sem.at[k, which * (depth // strip) + i],
            )
            for which, one in enumerate((w_ref, v_ref))
            for i in range(depth // strip)
        ]

    for k in range(3 * sends + owns):
        for copy in copies(k):
            copy.start()
    for left, a_ref, b_ref in zip(lefts, ins[::2], ins[1::2]):
        left[:, :depth] = a_ref[...]
        left[:, depth:] = b_ref[...]

    def run(k, carry):
        for copy in copies(k):
            copy.wait()
        half = both.shape[0] // 2
        both[...] = jnp.dot(lefts[0][...], w_buf[k], preferred_element_type=jnp.float32)

        @pl.when(k == 0)
        def _():
            outs[0][:half, :] = both[:half, :].astype(jnp.bfloat16)
            outs[1][:half, :] = both[half:, :].astype(jnp.bfloat16)

        @pl.when(k == 1)
        def _():
            outs[0][half:, :] = both[half:, :].astype(jnp.bfloat16)
            outs[2][...] = both[:half, :]

        @pl.when(k == 2)
        def _():
            outs[1][half:, :] = both[:half, :].astype(jnp.bfloat16)
            outs[3][...] = both[half:, :]

        return carry

    if sends:
        lax.fori_loop(0, 3, run, 0)
    if owns:
        for copy in copies(3 * sends):
            copy.wait()
        outs[-1][...] = jnp.dot(lefts[-1][...], w_buf[3 * sends], preferred_element_type=jnp.float32)


def product(cols, now, before, weight, theirs):
    depth = weight.shape[0]
    width = weight.shape[1] // (SIDE * CORES)
    sends, owns = int(now is not None), int(before is not None)
    ins = (now or ()) + (before or ())
    rows = [one.shape[0] for one in ins[::2]]
    shapes = []
    if sends:
        shapes += [((rows[0], width), jnp.bfloat16)] * 2 + [((rows[0] // 2, width), jnp.float32)] * 2
    if owns:
        shapes += [((rows[-1], width), jnp.float32)]
    vmem = pl.BlockSpec(memory_space=pltpu.VMEM)
    hbm = pl.BlockSpec(memory_space=pltpu.HBM)
    steps = 3 * sends + owns
    return pl.pallas_call(
        functools.partial(product_kernel, sends, owns),
        out_shape=[jax.ShapeDtypeStruct(s, d) for s, d in shapes],
        in_specs=[pl.BlockSpec(memory_space=pltpu.SMEM)] + [vmem] * len(ins) + [hbm] * 2,
        out_specs=[vmem] * len(shapes),
        scratch_shapes=[pltpu.VMEM((one, 2 * depth), jnp.bfloat16) for one in rows]
        + [
            pltpu.VMEM((rows[0], width), jnp.float32),
            pltpu.VMEM((steps, 2 * depth, width), jnp.bfloat16),
            pltpu.SemaphoreType.DMA((steps, 8)),
        ],
        compiler_params=pltpu.CompilerParams(vmem_limit_bytes=(12 + 4 * steps) << 20),
        cost_estimate=cost(
            4 * rows[0] * depth * width * steps, 8 * rows[0] * width + 4 * depth * width * steps
        ),
        name="product",
    )(cols, *ins, in_hbm(weight), in_hbm(theirs))


def cost(flops, bytes_accessed):
    return pl.CostEstimate(flops=flops * 8 // COST, bytes_accessed=bytes_accessed // COST, transcendentals=0)


def after(value, *others):
    return lax.optimization_barrier((value,) + others)[0]


def body(queries, keys, values, key_blocks, block_counts, out_weight):
    tokens = queries.shape[0]
    seq_index = lax.axis_index("seq")
    tensor_index = lax.axis_index("tensor")
    y, core = tensor_index // CORES, tensor_index % CORES
    kmax = key_blocks.shape[2]
    k_parts = gather(keys, along_x, along_z)
    v_parts = gather(values, along_z, along_x)
    plans = tables(key_blocks, block_counts, seq_index, tokens // BLOCK)

    cols = jnp.stack([(y + step) % SIDE * CORES + core for step in ORDER]).astype(jnp.int32)
    theirs = lax.ppermute(after(out_weight, *k_parts[:2], *v_parts[:2]), "tensor", other_core())

    def send(piece, step):
        return lax.ppermute(piece, "tensor", along_y(step))

    def second(up, down, up_rest, down_rest):
        half = up_rest.shape[0]
        low = (up_rest + up[:half].astype(jnp.float32)).astype(jnp.bfloat16)
        high = (down_rest + down[:half].astype(jnp.float32)).astype(jnp.bfloat16)
        return low, high

    def finish(own, up, down, up_low, down_high):
        half = own.shape[0] // 2
        low = own[:half] + up_low.astype(jnp.float32) + down[half:].astype(jnp.float32)
        high = own[half:] + up[half:].astype(jnp.float32) + down_high.astype(jnp.float32)
        return [low.astype(jnp.bfloat16), high.astype(jnp.bfloat16)]

    results = []
    at = 0
    before, settled = None, ()
    for blocks, plan in zip(CHUNKS, plans):
        some = queries[at : at + blocks * BLOCK]
        at += blocks * BLOCK
        if before is None:
            attended, key_all, value_all = attend(plan, some, kmax, k_parts, v_parts)
        else:
            attended = attend(after(plan, up_rest, *settled), some, kmax, [key_all], [value_all])
        swapped = lax.ppermute(attended, "tensor", other_core())
        if before is None:
            made = product(cols, (attended, swapped), None, out_weight, theirs)
        else:
            low, high = second(up, down, up_rest, down_rest)
            pair = after(attended, low, high), swapped
            low, high = send(low, 1), send(high, -1)
            *made, own = product(cols, pair, before, out_weight, theirs)
            results += finish(own, up, down, low, high)
            settled = low, high
        up, down, up_rest, down_rest = made
        up, down = send(up, 1), send(down, -1)
        before = attended, swapped
    (own,) = product(cols, None, before, out_weight, theirs)
    low, high = second(up, down, up_rest, down_rest)
    results += finish(own, up, down, send(low, 1), send(high, -1))
    return jnp.concatenate(results, 0)


def solution(mesh):
    placed = (
        P("seq", "tensor"),
        P("seq", "tensor"),
        P("seq", "tensor"),
        P("tensor", None, None),
        P("tensor", None),
        P("tensor", None),
    )
    return jax.shard_map(
        body, mesh=mesh, in_specs=placed, out_specs=P("seq", "tensor"), check_vma=False
    )
```

```python
import functools
import math

import jax
import jax.numpy as jnp
from jax import lax
from jax.experimental import pallas as pl
from jax.experimental.pallas import tpu as pltpu
from jax.sharding import PartitionSpec as P

HEAD_DIM = 128
BLOCK = 128
SIDE = 4
CORES = 2
PARTS = 8
CHUNKS = (4, 4)
VARIANTS = (1, 2, 3, 4, 6, 8)
ORDER = (2, 1, 3, 0)
COST = 2
NEG = -1e30


def along_x(step):
    return [(z * SIDE + x, z * SIDE + (x + step) % SIDE) for z in range(SIDE) for x in range(SIDE)]


def along_z(step):
    return [(z * SIDE + x, (z + step) % SIDE * SIDE + x) for z in range(SIDE) for x in range(SIDE)]


def along_y(step):
    return [(y * CORES + c, (y + step) % SIDE * CORES + c) for y in range(SIDE) for c in range(CORES)]


def other_core():
    return [(y * CORES + c, y * CORES + CORES - 1 - c) for y in range(SIDE) for c in range(CORES)]


def ring(piece, perm):
    half = piece.shape[0] // 2
    before = lax.ppermute(piece, "seq", perm(1))
    after = lax.ppermute(piece, "seq", perm(-1))
    far_low = lax.ppermute(before[:half], "seq", perm(1))
    far_high = lax.ppermute(after[half:], "seq", perm(-1))
    return before, after, far_low, far_high


def gather(piece, first, second):
    before, behind, far_low, far_high = ring(piece, first)
    low = jnp.concatenate([piece, before], 0)
    high = jnp.concatenate([behind, far_low, far_high], 0)

    def pass_on(part, step):
        return lax.ppermute(part, "seq", second(step))

    low_before, high_behind = pass_on(low, 1), pass_on(high, -1)
    low_behind, high_before = pass_on(low, -1), pass_on(high, 1)
    low_far, high_far = pass_on(low_before, 1), pass_on(high_behind, -1)
    return [low, high, low_before, high_before, low_behind, high_behind, low_far, high_far]


def attend_first_kernel(kmax, tab, q_ref, *refs):
    parts, (o_ref, k_out, v_out), (k_all, v_all, sem) = refs[: 2 * PARTS], refs[2 * PARTS : -3], refs[-3:]
    copies = []
    for some, whole in ((parts[:PARTS], k_all), (parts[PARTS:], v_all)):
        at = 0
        for part in some:
            copies.append(pltpu.make_async_copy(part, whole.at[pl.ds(at, part.shape[0])], sem.at[len(copies)]))
            at += part.shape[0]
    for copy in copies:
        copy.start()
    for copy in copies:
        copy.wait()
    keep = [
        pltpu.make_async_copy(k_all, k_out, sem.at[2 * PARTS]),
        pltpu.make_async_copy(v_all, v_out, sem.at[2 * PARTS + 1]),
    ]
    for copy in keep:
        copy.start()
    attend_kernel(kmax, tab, q_ref, k_all, v_all, o_ref)
    for copy in keep:
        copy.wait()


def attend_kernel(kmax, tab, q_ref, k_all, v_all, o_ref):
    heads = q_ref.shape[1] // HEAD_DIM
    units = q_ref.shape[0] // BLOCK * heads
    counts_at, keys_at, values_at = units, 2 * units, 2 * units + units * kmax
    scale = HEAD_DIM ** -0.5 * math.log2(math.e)
    rows = lax.broadcasted_iota(jnp.int32, (BLOCK, BLOCK), 0)
    cols = lax.broadcasted_iota(jnp.int32, (BLOCK, BLOCK), 1)
    causal = rows >= cols

    def block_of(ref, slot):
        return ref[pl.ds(pl.multiple_of(slot * BLOCK, BLOCK), BLOCK), :]

    def unit_scores(unit, pairs):
        head, local = unit % heads, unit // heads
        q = q_ref[
            pl.ds(pl.multiple_of(local * BLOCK, BLOCK), BLOCK),
            pl.ds(pl.multiple_of(head * HEAD_DIM, HEAD_DIM), HEAD_DIM),
        ]
        count = tab[counts_at + unit]
        scores = []
        for pair in range(pairs):
            two = jnp.concatenate(
                [block_of(k_all, tab[keys_at + unit * kmax + 2 * pair + i]) for i in range(2)], 0
            )
            both = lax.dot_general(q, two, (((1,), (1,)), ((), ())), preferred_element_type=jnp.float32)
            for i in range(2):
                j = 2 * pair + i
                one = both[:, i * BLOCK : (i + 1) * BLOCK]
                if j == 0:
                    one = jnp.where(causal, one, NEG)
                else:
                    one = one + jnp.where(j < count, 0.0, NEG).astype(jnp.float32)
                scores.append(one)
        return scores

    def unit_weights(scores):
        top = functools.reduce(jnp.maximum, scores)
        top = jnp.max(top, axis=1, keepdims=True)
        weights = [jnp.exp2((one - top) * scale) for one in scores]
        total = functools.reduce(jnp.add, weights)
        total = jnp.sum(total, axis=1, keepdims=True)
        return [one.astype(jnp.bfloat16) for one in weights], total

    def unit_finish(unit, weights, total):
        head, local = unit % heads, unit // heads
        values = jnp.concatenate(
            [block_of(v_all, tab[values_at + unit * kmax + j]) for j in range(len(weights))], 0
        )
        acc = jnp.dot(jnp.concatenate(weights, 1), values, preferred_element_type=jnp.float32)
        o_ref[
            pl.ds(pl.multiple_of(local * BLOCK, BLOCK), BLOCK),
            pl.ds(pl.multiple_of(head * HEAD_DIM, HEAD_DIM), HEAD_DIM),
        ] = (acc / total).astype(jnp.bfloat16)

    def step(group, carry):
        members = [tab[2 * group + i] for i in range(2)]
        most = jnp.maximum(tab[counts_at + members[0]], tab[counts_at + members[1]])
        need = (most + 1) // 2
        fewer = 0
        for pairs in VARIANTS:

            @pl.when((need > fewer) & (need <= pairs))
            def _():
                scores = [unit_scores(unit, pairs) for unit in members]
                ready = [unit_weights(one) for one in scores]
                for unit, (weights, total) in zip(members, ready):
                    unit_finish(unit, weights, total)

            fewer = pairs
        return carry

    lax.fori_loop(0, units // 2, step, 0)


def in_hbm(array):
    return pltpu.with_memory_space_constraint(array, pltpu.HBM)


def in_vmem(array):
    return pltpu.with_memory_space_constraint(array, pltpu.VMEM)


def attend(table, queries, kmax, k_parts, v_parts):
    rows, width = queries.shape
    tokens = sum(part.shape[0] for part in k_parts)
    vmem = pl.BlockSpec(memory_space=pltpu.VMEM)
    smem = pl.BlockSpec(memory_space=pltpu.SMEM)
    pairs = rows // BLOCK * (width // HEAD_DIM) * kmax // 2
    declared = cost(pairs * 4 * BLOCK * BLOCK * HEAD_DIM, 4 * tokens * HEAD_DIM + 4 * rows * width)
    gathered = len(k_parts) > 1
    params = pltpu.CompilerParams(vmem_limit_bytes=(20 if gathered else 8) << 20)
    out = jax.ShapeDtypeStruct((rows, width), jnp.bfloat16)
    if gathered:
        hbm = pl.BlockSpec(memory_space=pltpu.HBM)
        whole = pltpu.HBM((tokens, HEAD_DIM), jnp.bfloat16)
        held = pltpu.VMEM((tokens, HEAD_DIM), jnp.bfloat16)
        return pl.pallas_call(
            functools.partial(attend_first_kernel, kmax),
            out_shape=[out, whole, whole],
            in_specs=[smem, vmem] + [hbm] * (2 * PARTS),
            out_specs=[vmem, hbm, hbm],
            scratch_shapes=[held, held, pltpu.SemaphoreType.DMA((2 * PARTS + 2,))],
            compiler_params=params,
            cost_estimate=declared,
            name="attend_first",
        )(table, queries, *map(in_hbm, k_parts), *map(in_hbm, v_parts))
    return pl.pallas_call(
        functools.partial(attend_kernel, kmax),
        out_shape=out,
        in_specs=[smem, vmem, vmem, vmem],
        out_specs=vmem,
        compiler_params=params,
        cost_estimate=declared,
        name="attend",
    )(table, queries, in_vmem(k_parts[0]), in_vmem(v_parts[0]))


def tables(key_blocks, block_counts, seq_index, local_blocks):
    heads, _, kmax = key_blocks.shape
    start = seq_index * local_blocks
    lists = lax.dynamic_slice_in_dim(key_blocks, start, local_blocks, 1)
    counts = lax.dynamic_slice_in_dim(block_counts, start, local_blocks, 1)
    source = lists // local_blocks
    within = lists % local_blocks

    def place(step):
        step = step % SIDE
        return jnp.where(step == 0, 0, jnp.where(step == SIDE - 1, 1, jnp.where(step == 1, 2, 3)))

    z_place = place(source // SIDE - seq_index // SIDE)
    x_place = place(source % SIDE - seq_index % SIDE)
    key_at = (z_place * SIDE + x_place) * local_blocks + within
    value_at = (x_place * SIDE + z_place) * local_blocks + within
    counts, key_at, value_at = (jnp.moveaxis(one, 1, 0) for one in (counts, key_at, value_at))
    counts, key_at, value_at = (one.reshape(-1) for one in (counts, key_at, value_at))
    chunk = [index for index, blocks in enumerate(CHUNKS) for _ in range(blocks * heads)]
    order = jnp.argsort(counts + (kmax + 1) * jnp.array(chunk, jnp.int32)).astype(jnp.int32)
    out, at = [], 0
    for blocks in CHUNKS:
        units = slice(at, at + blocks * heads)
        slots = slice(at * kmax, (at + blocks * heads) * kmax)
        out.append(jnp.concatenate([order[units] - at, counts[units], key_at[slots], value_at[slots]], 0))
        at += blocks * heads
    return lax.optimization_barrier(out)


def product_kernel(sends, owns, cols, *refs):
    ins, refs = refs[: 2 * (sends + owns)], refs[2 * (sends + owns) :]
    w_ref, v_ref = refs[:2]
    outs, (both, w_buf, sem), lefts = refs[2 : 2 + 4 * sends + owns], refs[-3:], refs[2 + 4 * sends + owns : -3]
    depth = ins[0].shape[1]
    width = w_buf.shape[2]
    strip = 2 * depth // sem.shape[1]
    first = 0 if sends else 3

    def copies(k):
        source = pl.ds(pl.multiple_of(cols[first + k] * width, width), width)
        return [
            pltpu.make_async_copy(
                one.at[pl.ds(i * strip, strip), source],
                w_buf.at[k, pl.ds(which * depth + i * strip, strip), :],
                sem.at[k, which * (depth // strip) + i],
            )
            for which, one in enumerate((w_ref, v_ref))
            for i in range(depth // strip)
        ]

    for k in range(3 * sends + owns):
        for copy in copies(k):
            copy.start()
    for left, a_ref, b_ref in zip(lefts, ins[::2], ins[1::2]):
        left[:, :depth] = a_ref[...]
        left[:, depth:] = b_ref[...]

    def run(k, carry):
        for copy in copies(k):
            copy.wait()
        half = both.shape[0] // 2
        both[...] = jnp.dot(lefts[0][...], w_buf[k], preferred_element_type=jnp.float32)

        @pl.when(k == 0)
        def _():
            outs[0][:half, :] = both[:half, :].astype(jnp.bfloat16)
            outs[1][:half, :] = both[half:, :].astype(jnp.bfloat16)

        @pl.when(k == 1)
        def _():
            outs[0][half:, :] = both[half:, :].astype(jnp.bfloat16)
            outs[2][...] = both[:half, :]

        @pl.when(k == 2)
        def _():
            outs[1][half:, :] = both[:half, :].astype(jnp.bfloat16)
            outs[3][...] = both[half:, :]

        return carry

    if sends:
        lax.fori_loop(0, 3, run, 0)
    if owns:
        for copy in copies(3 * sends):
            copy.wait()
        outs[-1][...] = jnp.dot(lefts[-1][...], w_buf[3 * sends], preferred_element_type=jnp.float32)


def product(cols, now, before, weight, theirs):
    depth = weight.shape[0]
    width = weight.shape[1] // (SIDE * CORES)
    sends, owns = int(now is not None), int(before is not None)
    ins = (now or ()) + (before or ())
    rows = [one.shape[0] for one in ins[::2]]
    shapes = []
    if sends:
        shapes += [((rows[0], width), jnp.bfloat16)] * 2 + [((rows[0] // 2, width), jnp.float32)] * 2
    if owns:
        shapes += [((rows[-1], width), jnp.float32)]
    vmem = pl.BlockSpec(memory_space=pltpu.VMEM)
    hbm = pl.BlockSpec(memory_space=pltpu.HBM)
    steps = 3 * sends + owns
    return pl.pallas_call(
        functools.partial(product_kernel, sends, owns),
        out_shape=[jax.ShapeDtypeStruct(s, d) for s, d in shapes],
        in_specs=[pl.BlockSpec(memory_space=pltpu.SMEM)] + [vmem] * len(ins) + [hbm] * 2,
        out_specs=[vmem] * len(shapes),
        scratch_shapes=[pltpu.VMEM((one, 2 * depth), jnp.bfloat16) for one in rows]
        + [
            pltpu.VMEM((rows[0], width), jnp.float32),
            pltpu.VMEM((steps, 2 * depth, width), jnp.bfloat16),
            pltpu.SemaphoreType.DMA((steps, 8)),
        ],
        compiler_params=pltpu.CompilerParams(vmem_limit_bytes=(12 + 4 * steps) << 20),
        cost_estimate=cost(
            4 * rows[0] * depth * width * steps, 8 * rows[0] * width + 4 * depth * width * steps
        ),
        name="product",
    )(cols, *ins, in_hbm(weight), in_hbm(theirs))


def cost(flops, bytes_accessed):
    return pl.CostEstimate(flops=flops * 8 // COST, bytes_accessed=bytes_accessed // COST, transcendentals=0)


def after(value, *others):
    return lax.optimization_barrier((value,) + others)[0]


def body(queries, keys, values, key_blocks, block_counts, out_weight):
    tokens = queries.shape[0]
    seq_index = lax.axis_index("seq")
    tensor_index = lax.axis_index("tensor")
    y, core = tensor_index // CORES, tensor_index % CORES
    kmax = key_blocks.shape[2]
    k_parts = gather(keys, along_x, along_z)
    v_parts = gather(values, along_z, along_x)
    plans = tables(key_blocks, block_counts, seq_index, tokens // BLOCK)

    cols = jnp.stack([(y + step) % SIDE * CORES + core for step in ORDER]).astype(jnp.int32)
    theirs = lax.ppermute(out_weight, "tensor", other_core())

    def send(piece, step):
        return lax.ppermute(piece, "tensor", along_y(step))

    def second(up, down, up_rest, down_rest):
        half = up_rest.shape[0]
        low = (up_rest + up[:half].astype(jnp.float32)).astype(jnp.bfloat16)
        high = (down_rest + down[:half].astype(jnp.float32)).astype(jnp.bfloat16)
        return low, high

    def finish(own, up, down, up_low, down_high):
        half = own.shape[0] // 2
        low = own[:half] + up_low.astype(jnp.float32) + down[half:].astype(jnp.float32)
        high = own[half:] + up[half:].astype(jnp.float32) + down_high.astype(jnp.float32)
        return [low.astype(jnp.bfloat16), high.astype(jnp.bfloat16)]

    results = []
    at = 0
    before, settled = None, ()
    for blocks, plan in zip(CHUNKS, plans):
        some = queries[at : at + blocks * BLOCK]
        at += blocks * BLOCK
        if before is None:
            attended, key_all, value_all = attend(plan, some, kmax, k_parts, v_parts)
        else:
            attended = attend(after(plan, up_rest, *settled), some, kmax, [key_all], [value_all])
        swapped = lax.ppermute(attended, "tensor", other_core())
        if before is None:
            made = product(cols, (attended, swapped), None, out_weight, theirs)
        else:
            low, high = second(up, down, up_rest, down_rest)
            pair = after(attended, low, high), swapped
            low, high = send(low, 1), send(high, -1)
            *made, own = product(cols, pair, before, out_weight, theirs)
            results += finish(own, up, down, low, high)
            settled = low, high
        up, down, up_rest, down_rest = made
        up, down = send(up, 1), send(down, -1)
        before = attended, swapped
    (own,) = product(cols, None, before, out_weight, theirs)
    low, high = second(up, down, up_rest, down_rest)
    results += finish(own, up, down, send(low, 1), send(high, -1))
    return jnp.concatenate(results, 0)


def solution(mesh):
    placed = (
        P("seq", "tensor"),
        P("seq", "tensor"),
        P("seq", "tensor"),
        P("tensor", None, None),
        P("tensor", None),
        P("tensor", None),
    )
    return jax.shard_map(
        body, mesh=mesh, in_specs=placed, out_specs=P("seq", "tensor"), check_vma=False
    )
```

```python
import functools
import math

import jax
import jax.numpy as jnp
from jax import lax
from jax.experimental import pallas as pl
from jax.experimental.pallas import tpu as pltpu
from jax.sharding import PartitionSpec as P

HEAD_DIM = 128
BLOCK = 128
SIDE = 4
CORES = 2
PARTS = 8
CHUNKS = (4, 4)
VARIANTS = (1, 2, 3, 4, 6, 8)
ORDER = (2, 1, 3, 0)
COST = 2
NEG = -1e30


def along_x(step):
    return [(z * SIDE + x, z * SIDE + (x + step) % SIDE) for z in range(SIDE) for x in range(SIDE)]


def along_z(step):
    return [(z * SIDE + x, (z + step) % SIDE * SIDE + x) for z in range(SIDE) for x in range(SIDE)]


def along_y(step):
    return [(y * CORES + c, (y + step) % SIDE * CORES + c) for y in range(SIDE) for c in range(CORES)]


def other_core():
    return [(y * CORES + c, y * CORES + CORES - 1 - c) for y in range(SIDE) for c in range(CORES)]


def ring(piece, perm):
    half = piece.shape[0] // 2
    before = lax.ppermute(piece, "seq", perm(1))
    after = lax.ppermute(piece, "seq", perm(-1))
    far_low = lax.ppermute(before[:half], "seq", perm(1))
    far_high = lax.ppermute(after[half:], "seq", perm(-1))
    return before, after, far_low, far_high


def gather(piece, first, second):
    before, behind, far_low, far_high = ring(piece, first)
    low = jnp.concatenate([piece, before], 0)
    high = jnp.concatenate([behind, far_low, far_high], 0)

    def pass_on(part, step):
        return lax.ppermute(part, "seq", second(step))

    low_before, high_behind = pass_on(low, 1), pass_on(high, -1)
    low_behind, high_before = pass_on(low, -1), pass_on(high, 1)
    low_far, high_far = pass_on(low_before, 1), pass_on(high_behind, -1)
    return [low, high, low_before, high_before, low_behind, high_behind, low_far, high_far]


def attend_first_kernel(kmax, tab, q_ref, *refs):
    parts, (o_ref, k_out, v_out), (k_all, v_all, sem) = refs[: 2 * PARTS], refs[2 * PARTS : -3], refs[-3:]
    copies = []
    for some, whole in ((parts[:PARTS], k_all), (parts[PARTS:], v_all)):
        at = 0
        for part in some:
            copies.append(pltpu.make_async_copy(part, whole.at[pl.ds(at, part.shape[0])], sem.at[len(copies)]))
            at += part.shape[0]
    for copy in copies:
        copy.start()
    for copy in copies:
        copy.wait()
    keep = [
        pltpu.make_async_copy(k_all, k_out, sem.at[2 * PARTS]),
        pltpu.make_async_copy(v_all, v_out, sem.at[2 * PARTS + 1]),
    ]
    for copy in keep:
        copy.start()
    attend_kernel(kmax, tab, q_ref, k_all, v_all, o_ref)
    for copy in keep:
        copy.wait()


def attend_kernel(kmax, tab, q_ref, k_all, v_all, o_ref):
    heads = q_ref.shape[1] // HEAD_DIM
    units = q_ref.shape[0] // BLOCK * heads
    counts_at, keys_at, values_at = units, 2 * units, 2 * units + units * kmax
    scale = HEAD_DIM ** -0.5 * math.log2(math.e)
    rows = lax.broadcasted_iota(jnp.int32, (BLOCK, BLOCK), 0)
    cols = lax.broadcasted_iota(jnp.int32, (BLOCK, BLOCK), 1)
    causal = rows >= cols

    def block_of(ref, slot):
        return ref[pl.ds(pl.multiple_of(slot * BLOCK, BLOCK), BLOCK), :]

    def unit_scores(unit, pairs):
        head, local = unit % heads, unit // heads
        q = q_ref[
            pl.ds(pl.multiple_of(local * BLOCK, BLOCK), BLOCK),
            pl.ds(pl.multiple_of(head * HEAD_DIM, HEAD_DIM), HEAD_DIM),
        ]
        count = tab[counts_at + unit]
        scores = []
        for pair in range(pairs):
            two = jnp.concatenate(
                [block_of(k_all, tab[keys_at + unit * kmax + 2 * pair + i]) for i in range(2)], 0
            )
            both = lax.dot_general(q, two, (((1,), (1,)), ((), ())), preferred_element_type=jnp.float32)
            for i in range(2):
                j = 2 * pair + i
                one = both[:, i * BLOCK : (i + 1) * BLOCK]
                if j == 0:
                    one = jnp.where(causal, one, NEG)
                else:
                    one = one + jnp.where(j < count, 0.0, NEG).astype(jnp.float32)
                scores.append(one)
        return scores

    def unit_weights(scores):
        top = functools.reduce(jnp.maximum, scores)
        top = jnp.max(top, axis=1, keepdims=True)
        weights = [jnp.exp2((one - top) * scale) for one in scores]
        total = functools.reduce(jnp.add, weights)
        total = jnp.sum(total, axis=1, keepdims=True)
        return [one.astype(jnp.bfloat16) for one in weights], total

    def unit_finish(unit, weights, total):
        head, local = unit % heads, unit // heads
        values = jnp.concatenate(
            [block_of(v_all, tab[values_at + unit * kmax + j]) for j in range(len(weights))], 0
        )
        acc = jnp.dot(jnp.concatenate(weights, 1), values, preferred_element_type=jnp.float32)
        o_ref[
            pl.ds(pl.multiple_of(local * BLOCK, BLOCK), BLOCK),
            pl.ds(pl.multiple_of(head * HEAD_DIM, HEAD_DIM), HEAD_DIM),
        ] = (acc / total).astype(jnp.bfloat16)

    def step(group, carry):
        members = [tab[2 * group + i] for i in range(2)]
        most = jnp.maximum(tab[counts_at + members[0]], tab[counts_at + members[1]])
        need = (most + 1) // 2
        fewer = 0
        for pairs in VARIANTS:

            @pl.when((need > fewer) & (need <= pairs))
            def _():
                scores = [unit_scores(unit, pairs) for unit in members]
                ready = [unit_weights(one) for one in scores]
                for unit, (weights, total) in zip(members, ready):
                    unit_finish(unit, weights, total)

            fewer = pairs
        return carry

    lax.fori_loop(0, units // 2, step, 0)


def in_hbm(array):
    return pltpu.with_memory_space_constraint(array, pltpu.HBM)


def in_vmem(array):
    return pltpu.with_memory_space_constraint(array, pltpu.VMEM)


def attend(table, queries, kmax, k_parts, v_parts):
    rows, width = queries.shape
    tokens = sum(part.shape[0] for part in k_parts)
    vmem = pl.BlockSpec(memory_space=pltpu.VMEM)
    smem = pl.BlockSpec(memory_space=pltpu.SMEM)
    pairs = rows // BLOCK * (width // HEAD_DIM) * kmax // 2
    declared = cost(pairs * 4 * BLOCK * BLOCK * HEAD_DIM, 4 * tokens * HEAD_DIM + 4 * rows * width)
    gathered = len(k_parts) > 1
    params = pltpu.CompilerParams(vmem_limit_bytes=(20 if gathered else 8) << 20)
    out = jax.ShapeDtypeStruct((rows, width), jnp.bfloat16)
    if gathered:
        hbm = pl.BlockSpec(memory_space=pltpu.HBM)
        whole = pltpu.HBM((tokens, HEAD_DIM), jnp.bfloat16)
        held = pltpu.VMEM((tokens, HEAD_DIM), jnp.bfloat16)
        return pl.pallas_call(
            functools.partial(attend_first_kernel, kmax),
            out_shape=[out, whole, whole],
            in_specs=[smem, vmem] + [hbm] * (2 * PARTS),
            out_specs=[vmem, hbm, hbm],
            scratch_shapes=[held, held, pltpu.SemaphoreType.DMA((2 * PARTS + 2,))],
            compiler_params=params,
            cost_estimate=declared,
            name="attend_first",
        )(table, queries, *map(in_hbm, k_parts), *map(in_hbm, v_parts))
    return pl.pallas_call(
        functools.partial(attend_kernel, kmax),
        out_shape=out,
        in_specs=[smem, vmem, vmem, vmem],
        out_specs=vmem,
        compiler_params=params,
        cost_estimate=declared,
        name="attend",
    )(table, queries, in_vmem(k_parts[0]), in_vmem(v_parts[0]))


def tables(key_blocks, block_counts, seq_index, local_blocks):
    heads, _, kmax = key_blocks.shape
    start = seq_index * local_blocks
    lists = lax.dynamic_slice_in_dim(key_blocks, start, local_blocks, 1)
    counts = lax.dynamic_slice_in_dim(block_counts, start, local_blocks, 1)
    source = lists // local_blocks
    within = lists % local_blocks

    def place(step):
        step = step % SIDE
        return jnp.where(step == 0, 0, jnp.where(step == SIDE - 1, 1, jnp.where(step == 1, 2, 3)))

    z_place = place(source // SIDE - seq_index // SIDE)
    x_place = place(source % SIDE - seq_index % SIDE)
    key_at = (z_place * SIDE + x_place) * local_blocks + within
    value_at = (x_place * SIDE + z_place) * local_blocks + within
    counts, key_at, value_at = (jnp.moveaxis(one, 1, 0) for one in (counts, key_at, value_at))
    counts, key_at, value_at = (one.reshape(-1) for one in (counts, key_at, value_at))
    chunk = [index for index, blocks in enumerate(CHUNKS) for _ in range(blocks * heads)]
    order = jnp.argsort(counts + (kmax + 1) * jnp.array(chunk, jnp.int32)).astype(jnp.int32)
    out, at = [], 0
    for blocks in CHUNKS:
        units = slice(at, at + blocks * heads)
        slots = slice(at * kmax, (at + blocks * heads) * kmax)
        out.append(jnp.concatenate([order[units] - at, counts[units], key_at[slots], value_at[slots]], 0))
        at += blocks * heads
    return lax.optimization_barrier(out)


def product_kernel(sends, owns, cols, *refs):
    ins, refs = refs[: 2 * (sends + owns)], refs[2 * (sends + owns) :]
    w_ref, v_ref = refs[:2]
    outs, (both, w_buf, sem), lefts = refs[2 : 2 + 4 * sends + owns], refs[-3:], refs[2 + 4 * sends + owns : -3]
    depth = ins[0].shape[1]
    width = w_buf.shape[2]
    strip = 2 * depth // sem.shape[1]
    first = 0 if sends else 3

    def copies(k):
        source = pl.ds(pl.multiple_of(cols[first + k] * width, width), width)
        return [
            pltpu.make_async_copy(
                one.at[pl.ds(i * strip, strip), source],
                w_buf.at[k, pl.ds(which * depth + i * strip, strip), :],
                sem.at[k, which * (depth // strip) + i],
            )
            for which, one in enumerate((w_ref, v_ref))
            for i in range(depth // strip)
        ]

    for k in range(3 * sends + owns):
        for copy in copies(k):
            copy.start()
    for left, a_ref, b_ref in zip(lefts, ins[::2], ins[1::2]):
        left[:, :depth] = a_ref[...]
        left[:, depth:] = b_ref[...]

    def run(k, carry):
        for copy in copies(k):
            copy.wait()
        half = both.shape[0] // 2
        both[...] = jnp.dot(lefts[0][...], w_buf[k], preferred_element_type=jnp.float32)

        @pl.when(k == 0)
        def _():
            outs[0][:half, :] = both[:half, :].astype(jnp.bfloat16)
            outs[1][:half, :] = both[half:, :].astype(jnp.bfloat16)

        @pl.when(k == 1)
        def _():
            outs[0][half:, :] = both[half:, :].astype(jnp.bfloat16)
            outs[2][...] = both[:half, :]

        @pl.when(k == 2)
        def _():
            outs[1][half:, :] = both[:half, :].astype(jnp.bfloat16)
            outs[3][...] = both[half:, :]

        return carry

    if sends:
        lax.fori_loop(0, 3, run, 0)
    if owns:
        for copy in copies(3 * sends):
            copy.wait()
        outs[-1][...] = jnp.dot(lefts[-1][...], w_buf[3 * sends], preferred_element_type=jnp.float32)


def product(cols, now, before, weight, theirs):
    depth = weight.shape[0]
    width = weight.shape[1] // (SIDE * CORES)
    sends, owns = int(now is not None), int(before is not None)
    ins = (now or ()) + (before or ())
    rows = [one.shape[0] for one in ins[::2]]
    shapes = []
    if sends:
        shapes += [((rows[0], width), jnp.bfloat16)] * 2 + [((rows[0] // 2, width), jnp.float32)] * 2
    if owns:
        shapes += [((rows[-1], width), jnp.float32)]
    vmem = pl.BlockSpec(memory_space=pltpu.VMEM)
    hbm = pl.BlockSpec(memory_space=pltpu.HBM)
    steps = 3 * sends + owns
    return pl.pallas_call(
        functools.partial(product_kernel, sends, owns),
        out_shape=[jax.ShapeDtypeStruct(s, d) for s, d in shapes],
        in_specs=[pl.BlockSpec(memory_space=pltpu.SMEM)] + [vmem] * len(ins) + [hbm] * 2,
        out_specs=[vmem] * len(shapes),
        scratch_shapes=[pltpu.VMEM((one, 2 * depth), jnp.bfloat16) for one in rows]
        + [
            pltpu.VMEM((rows[0], width), jnp.float32),
            pltpu.VMEM((steps, 2 * depth, width), jnp.bfloat16),
            pltpu.SemaphoreType.DMA((steps, 8)),
        ],
        compiler_params=pltpu.CompilerParams(vmem_limit_bytes=(12 + 4 * steps) << 20),
        cost_estimate=cost(
            4 * rows[0] * depth * width * steps, 8 * rows[0] * width + 4 * depth * width * steps
        ),
        name="product",
    )(cols, *ins, in_hbm(weight), in_hbm(theirs))


def cost(flops, bytes_accessed):
    return pl.CostEstimate(flops=flops * 8 // COST, bytes_accessed=bytes_accessed // COST, transcendentals=0)


def after(value, *others):
    return lax.optimization_barrier((value,) + others)[0]


def body(queries, keys, values, key_blocks, block_counts, out_weight):
    tokens = queries.shape[0]
    seq_index = lax.axis_index("seq")
    tensor_index = lax.axis_index("tensor")
    y, core = tensor_index // CORES, tensor_index % CORES
    kmax = key_blocks.shape[2]
    k_parts = gather(keys, along_x, along_z)
    v_parts = gather(values, along_z, along_x)
    plans = tables(key_blocks, block_counts, seq_index, tokens // BLOCK)

    cols = jnp.stack([(y + step) % SIDE * CORES + core for step in ORDER]).astype(jnp.int32)
    theirs = lax.ppermute(out_weight, "tensor", other_core())

    def send(piece, step):
        return lax.ppermute(piece, "tensor", along_y(step))

    def second(up, down, up_rest, down_rest):
        half = up_rest.shape[0]
        low = (up_rest + up[:half].astype(jnp.float32)).astype(jnp.bfloat16)
        high = (down_rest + down[:half].astype(jnp.float32)).astype(jnp.bfloat16)
        return low, high

    def finish(own, up, down, up_low, down_high):
        half = own.shape[0] // 2
        low = own[:half] + up_low.astype(jnp.float32) + down[half:].astype(jnp.float32)
        high = own[half:] + up[half:].astype(jnp.float32) + down_high.astype(jnp.float32)
        return [low.astype(jnp.bfloat16), high.astype(jnp.bfloat16)]

    results = []
    at = 0
    before, settled = None, ()
    for blocks, plan in zip(CHUNKS, plans):
        some = queries[at : at + blocks * BLOCK]
        at += blocks * BLOCK
        if before is None:
            attended, key_all, value_all = attend(plan, some, kmax, k_parts, v_parts)
        else:
            attended = attend(after(plan, up_rest, *settled), some, kmax, [key_all], [value_all])
        swapped = lax.ppermute(attended, "tensor", other_core())
        if before is None:
            made = product(cols, (attended, swapped), None, out_weight, theirs)
        else:
            low, high = second(up, down, up_rest, down_rest)
            pair = after(attended, low, high), swapped
            low, high = send(low, 1), send(high, -1)
            *made, own = product(cols, pair, before, out_weight, theirs)
            results += finish(own, up, down, low, high)
            settled = low, high
        up, down, up_rest, down_rest = made
        up, down = send(up, 1), send(down, -1)
        before = attended, swapped
    before = after(before[0], *settled), before[1]
    (own,) = product(cols, None, before, out_weight, theirs)
    low, high = second(up, down, after(up_rest, own), after(down_rest, own))
    results += finish(own, up, down, send(low, 1), send(high, -1))
    return jnp.concatenate(results, 0)


def solution(mesh):
    placed = (
        P("seq", "tensor"),
        P("seq", "tensor"),
        P("seq", "tensor"),
        P("tensor", None, None),
        P("tensor", None),
        P("tensor", None),
    )
    return jax.shard_map(
        body, mesh=mesh, in_specs=placed, out_specs=P("seq", "tensor"), check_vma=False
    )
```

```python
import functools
import math

import jax
import jax.numpy as jnp
from jax import lax
from jax.experimental import pallas as pl
from jax.experimental.pallas import tpu as pltpu
from jax.sharding import PartitionSpec as P

HEAD_DIM = 128
BLOCK = 128
SIDE = 4
CORES = 2
PARTS = 8
CHUNKS = (4, 4)
VARIANTS = (1, 2, 3, 4, 5, 6, 8)
ORDER = (2, 1, 3, 0)
COST = 2
NEG = -1e30


def along_x(step):
    return [(z * SIDE + x, z * SIDE + (x + step) % SIDE) for z in range(SIDE) for x in range(SIDE)]


def along_z(step):
    return [(z * SIDE + x, (z + step) % SIDE * SIDE + x) for z in range(SIDE) for x in range(SIDE)]


def along_y(step):
    return [(y * CORES + c, (y + step) % SIDE * CORES + c) for y in range(SIDE) for c in range(CORES)]


def other_core():
    return [(y * CORES + c, y * CORES + CORES - 1 - c) for y in range(SIDE) for c in range(CORES)]


def ring(piece, perm):
    half = piece.shape[0] // 2
    before = lax.ppermute(piece, "seq", perm(1))
    after = lax.ppermute(piece, "seq", perm(-1))
    far_low = lax.ppermute(before[:half], "seq", perm(1))
    far_high = lax.ppermute(after[half:], "seq", perm(-1))
    return before, after, far_low, far_high


def gather(piece, first, second):
    before, behind, far_low, far_high = ring(piece, first)
    low = jnp.concatenate([piece, before], 0)
    high = jnp.concatenate([behind, far_low, far_high], 0)

    def pass_on(part, step):
        return lax.ppermute(part, "seq", second(step))

    low_before, high_behind = pass_on(low, 1), pass_on(high, -1)
    low_behind, high_before = pass_on(low, -1), pass_on(high, 1)
    low_far, high_far = pass_on(low_before, 1), pass_on(high_behind, -1)
    return [low, high, low_before, high_before, low_behind, high_behind, low_far, high_far]


def attend_first_kernel(kmax, tab, q_ref, *refs):
    parts, (o_ref, k_out, v_out), (k_all, v_all, sem) = refs[: 2 * PARTS], refs[2 * PARTS : -3], refs[-3:]
    copies = []
    for some, whole in ((parts[:PARTS], k_all), (parts[PARTS:], v_all)):
        at = 0
        for part in some:
            copies.append(pltpu.make_async_copy(part, whole.at[pl.ds(at, part.shape[0])], sem.at[len(copies)]))
            at += part.shape[0]
    for copy in copies:
        copy.start()
    for copy in copies:
        copy.wait()
    keep = [
        pltpu.make_async_copy(k_all, k_out, sem.at[2 * PARTS]),
        pltpu.make_async_copy(v_all, v_out, sem.at[2 * PARTS + 1]),
    ]
    for copy in keep:
        copy.start()
    attend_kernel(kmax, tab, q_ref, k_all, v_all, o_ref)
    for copy in keep:
        copy.wait()


def attend_kernel(kmax, tab, q_ref, k_all, v_all, o_ref):
    heads = q_ref.shape[1] // HEAD_DIM
    units = q_ref.shape[0] // BLOCK * heads
    counts_at, keys_at, values_at = units, 2 * units, 2 * units + units * kmax
    scale = HEAD_DIM ** -0.5 * math.log2(math.e)
    rows = lax.broadcasted_iota(jnp.int32, (BLOCK, BLOCK), 0)
    cols = lax.broadcasted_iota(jnp.int32, (BLOCK, BLOCK), 1)
    causal = rows >= cols

    def block_of(ref, slot):
        return ref[pl.ds(pl.multiple_of(slot * BLOCK, BLOCK), BLOCK), :]

    def unit_scores(unit, pairs):
        head, local = unit % heads, unit // heads
        q = q_ref[
            pl.ds(pl.multiple_of(local * BLOCK, BLOCK), BLOCK),
            pl.ds(pl.multiple_of(head * HEAD_DIM, HEAD_DIM), HEAD_DIM),
        ]
        count = tab[counts_at + unit]
        scores = []
        for pair in range(pairs):
            two = jnp.concatenate(
                [block_of(k_all, tab[keys_at + unit * kmax + 2 * pair + i]) for i in range(2)], 0
            )
            both = lax.dot_general(q, two, (((1,), (1,)), ((), ())), preferred_element_type=jnp.float32)
            for i in range(2):
                j = 2 * pair + i
                one = both[:, i * BLOCK : (i + 1) * BLOCK]
                if j == 0:
                    one = jnp.where(causal, one, NEG)
                else:
                    one = one + jnp.where(j < count, 0.0, NEG).astype(jnp.float32)
                scores.append(one)
        return scores

    def unit_weights(scores):
        top = functools.reduce(jnp.maximum, scores)
        top = jnp.max(top, axis=1, keepdims=True)
        weights = [jnp.exp2((one - top) * scale) for one in scores]
        total = functools.reduce(jnp.add, weights)
        total = jnp.sum(total, axis=1, keepdims=True)
        return [one.astype(jnp.bfloat16) for one in weights], total

    def unit_finish(unit, weights, total):
        head, local = unit % heads, unit // heads
        values = jnp.concatenate(
            [block_of(v_all, tab[values_at + unit * kmax + j]) for j in range(len(weights))], 0
        )
        acc = jnp.dot(jnp.concatenate(weights, 1), values, preferred_element_type=jnp.float32)
        o_ref[
            pl.ds(pl.multiple_of(local * BLOCK, BLOCK), BLOCK),
            pl.ds(pl.multiple_of(head * HEAD_DIM, HEAD_DIM), HEAD_DIM),
        ] = (acc / total).astype(jnp.bfloat16)

    def step(group, carry):
        members = [tab[2 * group + i] for i in range(2)]
        most = jnp.maximum(tab[counts_at + members[0]], tab[counts_at + members[1]])
        need = (most + 1) // 2
        fewer = 0
        for pairs in VARIANTS:

            @pl.when((need > fewer) & (need <= pairs))
            def _():
                scores = [unit_scores(unit, pairs) for unit in members]
                ready = [unit_weights(one) for one in scores]
                for unit, (weights, total) in zip(members, ready):
                    unit_finish(unit, weights, total)

            fewer = pairs
        return carry

    lax.fori_loop(0, units // 2, step, 0)


def in_hbm(array):
    return pltpu.with_memory_space_constraint(array, pltpu.HBM)


def in_vmem(array):
    return pltpu.with_memory_space_constraint(array, pltpu.VMEM)


def attend(table, queries, kmax, k_parts, v_parts):
    rows, width = queries.shape
    tokens = sum(part.shape[0] for part in k_parts)
    vmem = pl.BlockSpec(memory_space=pltpu.VMEM)
    smem = pl.BlockSpec(memory_space=pltpu.SMEM)
    pairs = rows // BLOCK * (width // HEAD_DIM) * kmax // 2
    declared = cost(pairs * 4 * BLOCK * BLOCK * HEAD_DIM, 4 * tokens * HEAD_DIM + 4 * rows * width)
    gathered = len(k_parts) > 1
    params = pltpu.CompilerParams(vmem_limit_bytes=(20 if gathered else 8) << 20)
    out = jax.ShapeDtypeStruct((rows, width), jnp.bfloat16)
    if gathered:
        hbm = pl.BlockSpec(memory_space=pltpu.HBM)
        whole = pltpu.HBM((tokens, HEAD_DIM), jnp.bfloat16)
        held = pltpu.VMEM((tokens, HEAD_DIM), jnp.bfloat16)
        return pl.pallas_call(
            functools.partial(attend_first_kernel, kmax),
            out_shape=[out, whole, whole],
            in_specs=[smem, vmem] + [hbm] * (2 * PARTS),
            out_specs=[vmem, hbm, hbm],
            scratch_shapes=[held, held, pltpu.SemaphoreType.DMA((2 * PARTS + 2,))],
            compiler_params=params,
            cost_estimate=declared,
            name="attend_first",
        )(table, queries, *map(in_hbm, k_parts), *map(in_hbm, v_parts))
    return pl.pallas_call(
        functools.partial(attend_kernel, kmax),
        out_shape=out,
        in_specs=[smem, vmem, vmem, vmem],
        out_specs=vmem,
        compiler_params=params,
        cost_estimate=declared,
        name="attend",
    )(table, queries, in_vmem(k_parts[0]), in_vmem(v_parts[0]))


def tables(key_blocks, block_counts, seq_index, local_blocks):
    heads, _, kmax = key_blocks.shape
    start = seq_index * local_blocks
    lists = lax.dynamic_slice_in_dim(key_blocks, start, local_blocks, 1)
    counts = lax.dynamic_slice_in_dim(block_counts, start, local_blocks, 1)
    source = lists // local_blocks
    within = lists % local_blocks

    def place(step):
        step = step % SIDE
        return jnp.where(step == 0, 0, jnp.where(step == SIDE - 1, 1, jnp.where(step == 1, 2, 3)))

    z_place = place(source // SIDE - seq_index // SIDE)
    x_place = place(source % SIDE - seq_index % SIDE)
    key_at = (z_place * SIDE + x_place) * local_blocks + within
    value_at = (x_place * SIDE + z_place) * local_blocks + within
    counts, key_at, value_at = (jnp.moveaxis(one, 1, 0) for one in (counts, key_at, value_at))
    counts, key_at, value_at = (one.reshape(-1) for one in (counts, key_at, value_at))
    chunk = [index for index, blocks in enumerate(CHUNKS) for _ in range(blocks * heads)]
    order = jnp.argsort(counts + (kmax + 1) * jnp.array(chunk, jnp.int32)).astype(jnp.int32)
    out, at = [], 0
    for blocks in CHUNKS:
        units = slice(at, at + blocks * heads)
        slots = slice(at * kmax, (at + blocks * heads) * kmax)
        out.append(jnp.concatenate([order[units] - at, counts[units], key_at[slots], value_at[slots]], 0))
        at += blocks * heads
    return lax.optimization_barrier(out)


def product_kernel(sends, owns, cols, *refs):
    ins, refs = refs[: 2 * (sends + owns)], refs[2 * (sends + owns) :]
    w_ref, v_ref = refs[:2]
    outs, (both, w_buf, sem), lefts = refs[2 : 2 + 4 * sends + owns], refs[-3:], refs[2 + 4 * sends + owns : -3]
    depth = ins[0].shape[1]
    width = w_buf.shape[2]
    strip = 2 * depth // sem.shape[1]
    first = 0 if sends else 3

    def copies(k):
        source = pl.ds(pl.multiple_of(cols[first + k] * width, width), width)
        return [
            pltpu.make_async_copy(
                one.at[pl.ds(i * strip, strip), source],
                w_buf.at[k, pl.ds(which * depth + i * strip, strip), :],
                sem.at[k, which * (depth // strip) + i],
            )
            for which, one in enumerate((w_ref, v_ref))
            for i in range(depth // strip)
        ]

    for k in range(3 * sends + owns):
        for copy in copies(k):
            copy.start()
    for left, a_ref, b_ref in zip(lefts, ins[::2], ins[1::2]):
        left[:, :depth] = a_ref[...]
        left[:, depth:] = b_ref[...]

    def run(k, carry):
        for copy in copies(k):
            copy.wait()
        half = both.shape[0] // 2
        both[...] = jnp.dot(lefts[0][...], w_buf[k], preferred_element_type=jnp.float32)

        @pl.when(k == 0)
        def _():
            outs[0][:half, :] = both[:half, :].astype(jnp.bfloat16)
            outs[1][:half, :] = both[half:, :].astype(jnp.bfloat16)

        @pl.when(k == 1)
        def _():
            outs[0][half:, :] = both[half:, :].astype(jnp.bfloat16)
            outs[2][...] = both[:half, :]

        @pl.when(k == 2)
        def _():
            outs[1][half:, :] = both[:half, :].astype(jnp.bfloat16)
            outs[3][...] = both[half:, :]

        return carry

    if sends:
        lax.fori_loop(0, 3, run, 0)
    if owns:
        for copy in copies(3 * sends):
            copy.wait()
        outs[-1][...] = jnp.dot(lefts[-1][...], w_buf[3 * sends], preferred_element_type=jnp.float32)


def product(cols, now, before, weight, theirs):
    depth = weight.shape[0]
    width = weight.shape[1] // (SIDE * CORES)
    sends, owns = int(now is not None), int(before is not None)
    ins = (now or ()) + (before or ())
    rows = [one.shape[0] for one in ins[::2]]
    shapes = []
    if sends:
        shapes += [((rows[0], width), jnp.bfloat16)] * 2 + [((rows[0] // 2, width), jnp.float32)] * 2
    if owns:
        shapes += [((rows[-1], width), jnp.float32)]
    vmem = pl.BlockSpec(memory_space=pltpu.VMEM)
    hbm = pl.BlockSpec(memory_space=pltpu.HBM)
    steps = 3 * sends + owns
    return pl.pallas_call(
        functools.partial(product_kernel, sends, owns),
        out_shape=[jax.ShapeDtypeStruct(s, d) for s, d in shapes],
        in_specs=[pl.BlockSpec(memory_space=pltpu.SMEM)] + [vmem] * len(ins) + [hbm] * 2,
        out_specs=[vmem] * len(shapes),
        scratch_shapes=[pltpu.VMEM((one, 2 * depth), jnp.bfloat16) for one in rows]
        + [
            pltpu.VMEM((rows[0], width), jnp.float32),
            pltpu.VMEM((steps, 2 * depth, width), jnp.bfloat16),
            pltpu.SemaphoreType.DMA((steps, 8)),
        ],
        compiler_params=pltpu.CompilerParams(vmem_limit_bytes=(12 + 4 * steps) << 20),
        cost_estimate=cost(
            4 * rows[0] * depth * width * steps, 8 * rows[0] * width + 4 * depth * width * steps
        ),
        name="product",
    )(cols, *ins, in_hbm(weight), in_hbm(theirs))


def cost(flops, bytes_accessed):
    return pl.CostEstimate(flops=flops * 8 // COST, bytes_accessed=bytes_accessed // COST, transcendentals=0)


def after(value, *others):
    return lax.optimization_barrier((value,) + others)[0]


def body(queries, keys, values, key_blocks, block_counts, out_weight):
    tokens = queries.shape[0]
    seq_index = lax.axis_index("seq")
    tensor_index = lax.axis_index("tensor")
    y, core = tensor_index // CORES, tensor_index % CORES
    kmax = key_blocks.shape[2]
    k_parts = gather(keys, along_x, along_z)
    v_parts = gather(values, along_z, along_x)
    plans = tables(key_blocks, block_counts, seq_index, tokens // BLOCK)

    cols = jnp.stack([(y + step) % SIDE * CORES + core for step in ORDER]).astype(jnp.int32)
    theirs = lax.ppermute(out_weight, "tensor", other_core())

    def send(piece, step):
        return lax.ppermute(piece, "tensor", along_y(step))

    def second(up, down, up_rest, down_rest):
        half = up_rest.shape[0]
        low = (up_rest + up[:half].astype(jnp.float32)).astype(jnp.bfloat16)
        high = (down_rest + down[:half].astype(jnp.float32)).astype(jnp.bfloat16)
        return low, high

    def finish(own, up, down, up_low, down_high):
        half = own.shape[0] // 2
        low = own[:half] + up_low.astype(jnp.float32) + down[half:].astype(jnp.float32)
        high = own[half:] + up[half:].astype(jnp.float32) + down_high.astype(jnp.float32)
        return [low.astype(jnp.bfloat16), high.astype(jnp.bfloat16)]

    results = []
    at = 0
    before, settled = None, ()
    for blocks, plan in zip(CHUNKS, plans):
        some = queries[at : at + blocks * BLOCK]
        at += blocks * BLOCK
        if before is None:
            attended, key_all, value_all = attend(plan, some, kmax, k_parts, v_parts)
        else:
            attended = attend(after(plan, up_rest, *settled), some, kmax, [key_all], [value_all])
        swapped = lax.ppermute(attended, "tensor", other_core())
        if before is None:
            made = product(cols, (attended, swapped), None, out_weight, theirs)
        else:
            low, high = second(up, down, up_rest, down_rest)
            pair = after(attended, low, high), swapped
            low, high = send(low, 1), send(high, -1)
            *made, own = product(cols, pair, before, out_weight, theirs)
            results += finish(own, up, down, low, high)
            settled = low, high
        up, down, up_rest, down_rest = made
        up, down = send(up, 1), send(down, -1)
        before = attended, swapped
    before = after(before[0], *settled), before[1]
    (own,) = product(cols, None, before, out_weight, theirs)
    low, high = second(up, down, after(up_rest, own), after(down_rest, own))
    results += finish(own, up, down, send(low, 1), send(high, -1))
    return jnp.concatenate(results, 0)


def solution(mesh):
    placed = (
        P("seq", "tensor"),
        P("seq", "tensor"),
        P("seq", "tensor"),
        P("tensor", None, None),
        P("tensor", None),
        P("tensor", None),
    )
    return jax.shard_map(
        body, mesh=mesh, in_specs=placed, out_specs=P("seq", "tensor"), check_vma=False
    )
```
